128 devices in a mesh: ctx: 16 (over y, x_hi, core), tp: 8 (over x_lo, z).
Axes of the slice: x: 4 (x_hi: 2, x_lo: 2; x = x_hi * 2 + x_lo), y: 4, z: 4, core: 2. Of those that a mesh axis runs over, the one named last changes fastest.
Arguments:
- query: bfloat16 [16384, 4096], P('ctx', 'tp'), may hold values from -6 to 6
- keys: bfloat16 [16384, 4096], P('ctx', 'tp'), may hold values from -6 to 6
- values: bfloat16 [16384, 4096], P('ctx', 'tp'), may hold values from -6 to 6
- residues: float32 [256, 16], replicated, may hold values from -1.5 to 1.5
- rates: float32 [256, 16], replicated, as said below
- w_out: bfloat16 [4096, 4096], P('tp'), may hold values from -0.125 to 0.125
Outputs:
- mixed: bfloat16 [16384, 4096], P('ctx', 'tp')
The draws below stay inside these ranges and needn't reach their ends.
Inputs may be any that keep to these rules, and one draw needn't show every extreme that they name: `rates`: each rate lies between 0.25 / 16384 and 1 / 32.
All inputs are finite; a program needn't handle non-finite values.
Results may differ from the reference program's by a relative error of at most 0.015.
Values may be sent and summed in bfloat16 or wider, within the bound.
No kernel may reach another device: no remote copies, remote signals or barrier semaphores. Data moves between devices by JAX's collectives and lax.ppermute only.
A program may use at most 64 MiB of HBM per device.

```python
import math
import jax
import jax.numpy as jnp
from jax import lax

D = 4096
SHARE = 16
STATE = 16
GROUPS = 256
LENGTH = 16384


def draw_rates(key, part):
    seeded = jax.random.fold_in(key, 7)
    pick_key, slow_key, fast_key = jax.random.split(seeded, 3)
    grid_shape = (GROUPS, STATE)
    lowest = math.log(0.25 / LENGTH)
    highest = math.log(1.0 / 32.0)
    middle = min(math.log(2.0 / LENGTH), highest)
    portion = 0.5
    chosen = jax.random.uniform(pick_key, grid_shape, jnp.float32) < portion
    slow_log = jax.random.uniform(slow_key, grid_shape, jnp.float32, lowest, middle)
    fast_log = jax.random.uniform(fast_key, grid_shape, jnp.float32, middle, highest)
    return jnp.exp(jnp.where(chosen, slow_log, fast_log)).astype(jnp.float32)


def spiked(result, key, source, target, blocks, factor):
    owner, partner = [(jnp.arange(result.shape[axis_at]) // (result.shape[axis_at] // blocks)).reshape([-1 if axis == axis_at else 1 for axis in range(result.ndim)]) for axis_at in (source, target)]
    chosen = jax.random.permutation(key, blocks)[partner]
    strong = (owner == chosen) | (owner == (partner + blocks // 2) % blocks)
    return jnp.where(strong, factor * result, result)


def shard_levels(rng, extent, cuts, least, top_value):
    loudness = 1.0
    for dim, blocks in cuts:
        heights = jax.random.uniform(jax.random.fold_in(jax.random.fold_in(rng, 6), dim), (blocks,), jnp.float32, least / len(cuts), top_value / len(cuts))
        loudness = loudness * jnp.repeat(jnp.exp(heights), extent[dim] // blocks).reshape((-1,) + (1,) * (len(extent) - 1 - dim))
    return loudness


def scatter_about(rng, dims, spread, bound, shards=(), kind=jnp.bfloat16):
    result = jax.random.normal(rng, dims, jnp.float32) * spread
    if len(shards) > 0:
        result = shard_levels(rng, dims, shards, -0.22, 0.18) * result
    return jnp.clip(result, min=-bound, max=bound).astype(kind)


def noise_with(own_key, extent, deviation, limit, pieces, heavy, kind=jnp.bfloat16):
    values = deviation * jax.random.normal(own_key, extent, jnp.float32)
    if pieces:
        values = values * shard_levels(own_key, extent, pieces, -0.22, 0.18)
    return jnp.clip(spiked(values, jax.random.fold_in(own_key, 3), *heavy), -limit, limit).astype(kind)


def setup_inputs(seed: int = 0) -> dict:
    arg_keys = jax.random.split(jax.random.key(seed), 7)
    query = scatter_about(arg_keys[0], (LENGTH, D), 1.0, 6.0, ((0, 16), (1, 8)))
    keys = scatter_about(arg_keys[1], (LENGTH, D), 1.0, 6.0, ((0, 16), (1, 8)))
    values = scatter_about(arg_keys[2], (LENGTH, D), 1.0, 6.0, ((0, 16), (1, 8)))
    residues = scatter_about(arg_keys[3], (GROUPS, STATE), STATE ** -0.5, 1.5, (), jnp.float32)
    rates = draw_rates(jax.random.fold_in(arg_keys[6], 71), 0)
    w_out = noise_with(arg_keys[5], (D, D), D ** -0.5, 0.125, ((0, 8),), (0, 1, 8, 2.0))
    return {"query": query, "keys": keys, "values": values, "residues": residues, "rates": rates, "w_out": w_out}


def modal_filter(residues, rates, count):
    position = jnp.arange(count, dtype=jnp.float32)
    mode_gain = residues * jnp.sqrt(2.0 * rates)
    fading = jnp.exp(-rates[:, :, None] * position[None, None, :])
    return jnp.einsum('gs,gst->tg', mode_gain, fading)

def reference(query, keys, values, residues, rates, w_out):
    product = (keys.astype(jnp.float32) * values.astype(jnp.float32)).astype(jnp.bfloat16)
    product = lax.optimization_barrier(product)
    kernel = modal_filter(residues, rates, LENGTH)
    grouped = product.astype(jnp.float32).reshape(LENGTH, GROUPS, SHARE).transpose(1, 0, 2)

    def per_group(member):
        signal, taps = member
        padded = 2 * LENGTH
        spectrum = jnp.fft.rfft(signal, n=padded, axis=0) * jnp.fft.rfft(taps, n=padded)[:, None]
        return jnp.fft.irfft(spectrum, n=padded, axis=0)[:LENGTH]
    folded = lax.map(per_group, (grouped, kernel.T))
    convolved = folded.transpose(1, 0, 2).reshape(LENGTH, D).astype(jnp.bfloat16)
    convolved = lax.optimization_barrier(convolved)
    gated = (query.astype(jnp.float32) * convolved.astype(jnp.float32)).astype(jnp.bfloat16)
    return jnp.dot(gated, w_out, preferred_element_type=jnp.float32).astype(jnp.bfloat16)
```

```python
import functools
import jax
import jax.numpy as jnp
from jax import lax
from jax.experimental import pallas as pl
from jax.sharding import PartitionSpec as P
from jax.experimental.pallas import tpu as pltpu

SHARE = 16
STATE = 16
CHUNK = 256
LANES = 128
PACK = LANES // SHARE


def pick(table, modes):
    return jnp.dot(table, modes, precision=lax.Precision.HIGHEST, preferred_element_type=jnp.float32)


def spread_modes(modes):
    groups = modes.shape[0]
    width = groups * SHARE
    owner = lax.broadcasted_iota(jnp.int32, (groups, width), 1) // SHARE
    table = (owner == lax.broadcasted_iota(jnp.int32, (groups, width), 0)).astype(jnp.float32)
    return lax.dot_general(
        modes, table, (((0,), (0,)), ((), ())),
        precision=lax.Precision.HIGHEST, preferred_element_type=jnp.float32,
    )


def as_row(spread):
    state = lax.broadcasted_iota(jnp.int32, spread.shape, 0)
    slot = lax.broadcasted_iota(jnp.int32, spread.shape, 1) % STATE
    return jnp.sum(jnp.where(state == slot, spread, 0.0), axis=0, keepdims=True)


def as_column(modes):
    groups = modes.shape[0]
    rows = groups * STATE
    owner = lax.broadcasted_iota(jnp.int32, (rows, groups), 0) // STATE
    table = (owner == lax.broadcasted_iota(jnp.int32, (rows, groups), 1)).astype(jnp.float32)
    wide = pick(table, modes)
    slot = lax.broadcasted_iota(jnp.int32, wide.shape, 0) % STATE
    state = lax.broadcasted_iota(jnp.int32, wide.shape, 1)
    return jnp.sum(jnp.where(state == slot, wide, 0.0), axis=1, keepdims=True)


def same_group():
    left = lax.broadcasted_iota(jnp.int32, (LANES, LANES), 0) // STATE
    right = lax.broadcasted_iota(jnp.int32, (LANES, LANES), 1) // SHARE
    return left == right


def state_kernel(rates_ref, keys_ref, values_ref, states_ref, last_ref, product_ref):
    length, width = keys_ref.shape
    chunks = length // CHUNK
    rates = rates_ref[...]
    spread = spread_modes(rates)
    column = as_column(rates)
    step = jnp.exp(-float(CHUNK) * spread)
    ahead = (CHUNK - 1 - lax.broadcasted_iota(jnp.int32, (LANES, CHUNK), 1)).astype(jnp.float32)
    keep = same_group()
    for block in range(width // LANES):
        lanes = pl.ds(block * LANES, LANES)
        fading = jnp.exp(-column[block * LANES : (block + 1) * LANES] * ahead).astype(jnp.bfloat16)
        decay = step[:, block * LANES : (block + 1) * LANES]
        carried = jnp.zeros((STATE, LANES), jnp.float32)
        for chunk in range(chunks):
            rows = pl.ds(chunk * CHUNK, CHUNK)
            product = (
                keys_ref[rows, lanes].astype(jnp.float32)
                * values_ref[rows, lanes].astype(jnp.float32)
            ).astype(jnp.bfloat16)
            product_ref[rows, lanes] = product
            full = jnp.dot(fading, product, preferred_element_type=jnp.float32)
            state = jnp.sum(
                jnp.where(keep, full, 0.0).reshape(PACK, STATE, LANES), axis=0
            )
            states_ref[pl.ds(chunk * STATE, STATE), lanes] = state
            carried = carried * decay + state
        last_ref[:, lanes] = carried


def local_kernel(rates_ref, residues_ref, product_ref, out_ref, turned_ref):
    length, width = product_ref.shape
    chunks = length // CHUNK
    rates = rates_ref[...]
    gains = residues_ref[...] * jnp.sqrt(2.0 * rates)
    rate_row = as_row(spread_modes(rates))
    gain_row = as_row(spread_modes(gains))
    column = as_column(rates)
    when = lax.broadcasted_iota(jnp.int32, (CHUNK, LANES), 0).astype(jnp.float32)
    ahead = lax.broadcasted_iota(jnp.int32, (LANES, CHUNK), 1).astype(jnp.float32)
    causal = lax.broadcasted_iota(jnp.int32, (CHUNK, CHUNK), 0) <= lax.broadcasted_iota(
        jnp.int32, (CHUNK, CHUNK), 1
    )
    member = lax.broadcasted_iota(jnp.int32, (LANES, CHUNK), 0) // STATE
    for block in range(width // LANES):
        cut = slice(block * LANES, (block + 1) * LANES)
        rising = (gain_row[:, cut] * jnp.exp(rate_row[:, cut] * when)).astype(jnp.bfloat16)
        fading = jnp.exp(-column[cut] * ahead)
        turned = product_ref[:, cut].T
        for group in range(PACK):
            own = jnp.where(member == group, fading, 0.0).astype(jnp.bfloat16)
            taps = jnp.dot(rising, own, preferred_element_type=jnp.float32)
            taps = jnp.where(causal, taps, 0.0).astype(jnp.bfloat16)
            rows = turned[group * SHARE : (group + 1) * SHARE]
            stacked = jnp.concatenate(
                [rows[:, c * CHUNK : (c + 1) * CHUNK] for c in range(chunks)], axis=0
            )
            folded = jnp.dot(stacked, taps, preferred_element_type=jnp.float32)
            for c in range(chunks):
                turned_ref[group * SHARE : (group + 1) * SHARE, c * CHUNK : (c + 1) * CHUNK] = (
                    folded[c * SHARE : (c + 1) * SHARE]
                )
        out_ref[:, cut] = turned_ref[...].T.astype(out_ref.dtype)


def gate_kernel(rates_ref, residues_ref, query_ref, local_ref, states_ref, entry_ref, out_ref):
    length, width = query_ref.shape
    chunks = length // CHUNK
    rates = rates_ref[...]
    gains = residues_ref[...] * jnp.sqrt(2.0 * rates)
    spread = spread_modes(rates)
    rate_row = as_row(spread)
    gain_row = as_row(spread_modes(gains))
    step = jnp.exp(-float(CHUNK) * spread)
    after = (1 + lax.broadcasted_iota(jnp.int32, (CHUNK, LANES), 0)).astype(jnp.float32)
    keep = same_group()
    for block in range(width // LANES):
        cut = slice(block * LANES, (block + 1) * LANES)
        fading = (gain_row[:, cut] * jnp.exp(-rate_row[:, cut] * after)).astype(jnp.bfloat16)
        carried = entry_ref[:, cut]
        for chunk in range(chunks):
            rows = slice(chunk * CHUNK, (chunk + 1) * CHUNK)
            tall = jnp.concatenate([carried] * PACK, axis=0)
            tall = jnp.where(keep, tall, 0.0).astype(jnp.bfloat16)
            earlier = jnp.dot(fading, tall, preferred_element_type=jnp.float32)
            convolved = (local_ref[rows, cut].astype(jnp.float32) + earlier).astype(jnp.bfloat16)
            out_ref[rows, cut] = (
                query_ref[rows, cut].astype(jnp.float32) * convolved.astype(jnp.float32)
            ).astype(jnp.bfloat16)
            carried = carried * step[:, cut] + states_ref[chunk * STATE : (chunk + 1) * STATE, cut]


def vmem():
    return pl.BlockSpec(memory_space=pltpu.VMEM)


def chunk_states(rates, keys, values):
    length, width = keys.shape
    return pl.pallas_call(
        state_kernel,
        out_shape=(
            jax.ShapeDtypeStruct((length // CHUNK * STATE, width), jnp.float32),
            jax.ShapeDtypeStruct((STATE, width), jnp.float32),
            jax.ShapeDtypeStruct((length, width), jnp.bfloat16),
        ),
        in_specs=[vmem()] * 3,
        out_specs=[vmem()] * 3,
    )(rates, keys, values)


def local_part(rates, residues, product):
    length, width = product.shape
    return pl.pallas_call(
        local_kernel,
        out_shape=jax.ShapeDtypeStruct((length, width), jnp.bfloat16),
        in_specs=[vmem()] * 3,
        out_specs=vmem(),
        scratch_shapes=[pltpu.VMEM((LANES, length), jnp.float32)],
    )(rates, residues, product)


def gate(rates, residues, query, local, states, entry):
    return pl.pallas_call(
        gate_kernel,
        out_shape=jax.ShapeDtypeStruct(query.shape, jnp.bfloat16),
        in_specs=[vmem()] * 6,
        out_specs=vmem(),
    )(rates, residues, query, local, states, entry)


def entry_state(rates, last):
    ctx = lax.axis_index("ctx")
    place = ctx % 4
    floor = ctx // 4
    spread = jnp.repeat(rates.T, SHARE, axis=1)
    length = 1024.0
    once = jnp.exp(-length * spread)
    two = jnp.exp(-2 * length * spread)
    three = jnp.exp(-3 * length * spread)
    four = jnp.exp(-4 * length * spread)
    eight = jnp.exp(-8 * length * spread)
    near = [last]
    for k in range(1, 4):
        near.append(lax.ppermute(last, "ctx", [(c, c // 4 * 4 + (c % 4 + k) % 4) for c in range(16)]))
    powers = [jnp.ones_like(once), once, two, three]
    total = jnp.zeros_like(last)
    before = jnp.zeros_like(last)
    for k in range(4):
        source = (place - k) % 4
        total = total + near[k] * jnp.exp(-length * (3 - source).astype(jnp.float32) * spread)
        if k:
            before = before + jnp.where(place >= k, powers[k - 1] * near[k], 0.0)
    above = jnp.zeros_like(last)
    for k in range(1, 4):
        got = lax.ppermute(total, "ctx", [(c, c + 4 * k) for c in range(16 - 4 * k)])
        above = above + got * (1.0, four, eight)[k - 1]
    return before + above * jnp.exp(-length * place.astype(jnp.float32) * spread)


def on_device(query, keys, values, residues, rates, w_out):
    groups = keys.shape[1] // SHARE
    first = lax.axis_index("tp") * groups
    rates = lax.dynamic_slice_in_dim(rates, first, groups, 0)
    residues = lax.dynamic_slice_in_dim(residues, first, groups, 0)
    states, last, product = chunk_states(rates, keys, values)
    local = local_part(rates, residues, product)
    entry = entry_state(rates, last)
    gated = gate(rates, residues, query, local, states, entry)
    partial = jnp.dot(gated, w_out, preferred_element_type=jnp.float32).astype(jnp.bfloat16)
    return lax.psum_scatter(partial, "tp", scatter_dimension=1, tiled=True)


def solution(mesh):
    in_specs = (P("ctx", "tp"), P("ctx", "tp"), P("ctx", "tp"), P(), P(), P("tp", None))
    out_specs = P("ctx", "tp")
    return jax.shard_map(
        on_device, mesh=mesh, in_specs=in_specs, out_specs=out_specs, check_vma=False
    )
```

```python
import functools
import jax
import jax.numpy as jnp
from jax import lax
from jax.experimental import pallas as pl
from jax.experimental.pallas import tpu as pltpu
from jax.sharding import PartitionSpec as P


SHARE = 16
STATE = 16
CHUNK = 128
PARTS = (128, 384)
EARLY = 96
LIMIT = 12 * 2**20
SPAN = 1024
LANES = 128
PACK = LANES // SHARE


def as_row(spread):
    state = lax.broadcasted_iota(jnp.int32, spread.shape, 0)
    slot = lax.broadcasted_iota(jnp.int32, spread.shape, 1) % STATE
    return jnp.sum(jnp.where(state == slot, spread, 0.0), axis=0, keepdims=True)


def same_group():
    left = lax.broadcasted_iota(jnp.int32, (LANES, LANES), 0) // STATE
    right = lax.broadcasted_iota(jnp.int32, (LANES, LANES), 1) // SHARE
    return left == right


def spread_modes(modes, width):
    groups = modes.shape[1]
    first = lax.axis_index("tp") * (width // SHARE)
    group = lax.broadcasted_iota(jnp.int32, (groups, width), 0) - first
    owner = lax.broadcasted_iota(jnp.int32, (groups, width), 1) // SHARE
    return exact_dot(modes, (group == owner).astype(jnp.float32), 0)


def exact_dot(left, right, side):
    return lax.dot_general(
        left, right, (((1,), (side,)), ((), ())),
        precision=lax.Precision.HIGHEST, preferred_element_type=jnp.float32,
    )


def as_column(modes, width):
    groups = modes.shape[1]
    first = lax.axis_index("tp") * (width // SHARE)
    group = lax.broadcasted_iota(jnp.int32, (width, groups), 1) - first
    owner = lax.broadcasted_iota(jnp.int32, (width, groups), 0) // STATE
    wide = exact_dot((group == owner).astype(jnp.float32), modes, 1)
    slot = lax.broadcasted_iota(jnp.int32, wide.shape, 0) % STATE
    state = lax.broadcasted_iota(jnp.int32, wide.shape, 1)
    return jnp.sum(jnp.where(state == slot, wide, 0.0), axis=1, keepdims=True)


def state_kernel(
    rates_hbm, residues_hbm, keys_hbm, values_hbm,
    states_ref, last_ref, spread_ref, leaving_ref, taps_ref, weights_ref,
    rates_ref, residues_ref, keys_ref, values_ref, sems,
):
    length, width = keys_ref.shape
    chunks = length // CHUNK
    copies = [
        pltpu.make_async_copy(source, target, sems.at[index])
        for index, (source, target) in enumerate(
            (
                (rates_hbm, rates_ref),
                (residues_hbm, residues_ref),
                (keys_hbm, keys_ref),
                (values_hbm, values_ref),
            )
        )
    ]
    for copy in copies:
        copy.start()
    copies[0].wait()
    copies[1].wait()
    rates = rates_ref[...]
    spread = spread_modes(rates, width)
    spread_ref[...] = spread
    column = as_column(rates, width)
    step = jnp.exp(-float(CHUNK) * spread)
    ahead = (CHUNK - 1 - lax.broadcasted_iota(jnp.int32, (LANES, CHUNK), 1)).astype(jnp.float32)
    keep = same_group()
    gains = residues_ref[...] * jnp.sqrt(2.0 * rates)
    rate_row = as_row(spread)
    gain_row = as_row(spread_modes(gains, width))
    after = (1 + lax.broadcasted_iota(jnp.int32, (CHUNK, width), 0)).astype(jnp.float32)
    leaving_ref[...] = (gain_row * jnp.exp(-rate_row * after)).astype(jnp.bfloat16)
    copies[2].wait()
    copies[3].wait()
    fadings = []
    for block in range(width // LANES):
        cut = slice(block * LANES, (block + 1) * LANES)
        fading = jnp.exp(-column[cut] * ahead)
        fadings.append(fading)
        fading = fading.astype(jnp.bfloat16)
        decay = step[:, cut]
        carried = jnp.zeros((STATE, LANES), jnp.float32)
        for chunk in range(chunks):
            rows = slice(chunk * CHUNK, (chunk + 1) * CHUNK)
            product = (
                keys_ref[rows, cut].astype(jnp.float32) * values_ref[rows, cut].astype(jnp.float32)
            ).astype(jnp.bfloat16)
            full = jnp.dot(fading, product, preferred_element_type=jnp.float32)
            state = jnp.sum(jnp.where(keep, full, 0.0).reshape(PACK, STATE, LANES), axis=0)
            states_ref[chunk * STATE : (chunk + 1) * STATE, cut] = state
            carried = carried * decay + state
        last_ref[:, cut] = carried
    causal = lax.broadcasted_iota(jnp.int32, (CHUNK, CHUNK), 0) >= lax.broadcasted_iota(
        jnp.int32, (CHUNK, CHUNK), 1
    )
    for block in range(width // LANES):
        cut = slice(block * LANES, (block + 1) * LANES)
        entering = (fadings[block] * jnp.exp(column[cut] * float(CHUNK))).astype(jnp.bfloat16)
        leaving = leaving_ref[:, cut]
        for group in range(PACK):
            at = group * SHARE
            rows = [entering[at : at + SHARE]]
            if group:
                rows.insert(0, jnp.zeros((at, CHUNK), jnp.bfloat16))
            if group < PACK - 1:
                rows.append(jnp.zeros((LANES - at - SHARE, CHUNK), jnp.bfloat16))
            taps = jnp.dot(
                leaving, jnp.concatenate(rows, axis=0), preferred_element_type=jnp.float32
            )
            index = block * PACK + group
            taps_ref[index * CHUNK : (index + 1) * CHUNK, :] = jnp.where(causal, taps, 0.0).astype(
                jnp.bfloat16
            )
    span = float(SPAN)
    mine = lax.axis_index("ctx") % 4
    for k in range(4):
        source = (mine - k) & 3
        weights_ref[k * STATE : (k + 1) * STATE, :] = jnp.exp(
            -span * (3 - source).astype(jnp.float32) * spread
        )
        if k:
            weights_ref[(k + 3) * STATE : (k + 4) * STATE, :] = jnp.where(
                mine >= k, jnp.exp(-span * (k - 1) * spread), 0.0
            )


def convolve_half(start, taps_ref, keys_ref, values_ref, turned_ref, put):
    rows = keys_ref.shape[0] // 2
    chunks = rows // CHUNK
    for block in range(keys_ref.shape[1] // LANES):
        cut = slice(block * LANES, (block + 1) * LANES)
        turned = (
            (
                keys_ref[pl.ds(start, rows), cut].astype(jnp.float32)
                * values_ref[pl.ds(start, rows), cut].astype(jnp.float32)
            )
            .astype(jnp.bfloat16)
            .T
        )
        for group in range(PACK):
            at = group * SHARE
            index = block * PACK + group
            stacked = jnp.concatenate(
                [turned[at : at + SHARE, c * CHUNK : (c + 1) * CHUNK] for c in range(chunks)], axis=0
            )
            folded = lax.dot_general(
                stacked,
                taps_ref[index * CHUNK : (index + 1) * CHUNK, :],
                (((1,), (1,)), ((), ())),
                preferred_element_type=jnp.float32,
            ).astype(jnp.bfloat16)
            for c in range(chunks):
                turned_ref[block, at : at + SHARE, c * CHUNK : (c + 1) * CHUNK] = (
                    folded[c * SHARE : (c + 1) * SHARE]
                )
        put(cut, turned_ref[block].T)


def gate_half(
    half, spread_ref, leaving_ref, query_ref, states_ref, before_ref, above_refs, local, put
):
    length, width = query_ref.shape
    chunks = length // CHUNK // 2
    span = float(SPAN)
    mine = lax.axis_index("ctx") % 4
    spread = spread_ref[...]
    step = jnp.exp(-float(CHUNK) * spread)
    group_step = jnp.exp(-4.0 * span * spread)
    one, two, three = [ref[...] for ref in above_refs]
    above = one + group_step * (two + group_step * three)
    entry = before_ref[...] + above * jnp.exp(-span * mine.astype(jnp.float32) * spread)
    keep = same_group()
    moved = entry
    for chunk in range(chunks):
        moved = moved * step + states_ref[chunk * STATE : (chunk + 1) * STATE, :]
    entry = jnp.where(half == 1, moved, entry)
    start = pl.multiple_of(half * (length // 2), length // 2)
    states = states_ref[pl.ds(pl.multiple_of(half * chunks * STATE, chunks * STATE), chunks * STATE), :]
    for block in range(width // LANES):
        cut = slice(block * LANES, (block + 1) * LANES)
        leaving = leaving_ref[:, cut]
        carried = entry[:, cut]
        near = local(cut)
        query = query_ref[pl.ds(start, length // 2), cut]
        for chunk in range(chunks):
            rows = slice(chunk * CHUNK, (chunk + 1) * CHUNK)
            tall = jnp.concatenate([carried] * PACK, axis=0)
            tall = jnp.where(keep, tall, 0.0).astype(jnp.bfloat16)
            earlier = jnp.dot(leaving, tall, preferred_element_type=jnp.float32)
            convolved = (near[rows].astype(jnp.float32) + earlier).astype(jnp.bfloat16)
            gated = query[rows].astype(jnp.float32) * convolved.astype(jnp.float32)
            put(chunk, cut, gated.astype(jnp.bfloat16))
            carried = carried * step[:, cut] + states[chunk * STATE : (chunk + 1) * STATE, cut]


def other_half():
    return 1 - lax.axis_index("tp") // 4


def near_kernel(taps_ref, keys_ref, values_ref, out_ref, turned_ref):
    rows = out_ref.shape[0]
    start = pl.multiple_of(other_half() * rows, rows)

    def put(cut, value):
        out_ref[:, cut] = value

    convolve_half(start, taps_ref, keys_ref, values_ref, turned_ref, put)


def send_kernel(
    spread_ref, leaving_ref, query_ref, near_ref, states_ref, before_ref,
    one_ref, two_ref, three_ref, *out_refs,
):
    homes = [(ref, row) for ref in out_refs for row in range(0, ref.shape[0], CHUNK)]

    def put(chunk, cut, value):
        ref, row = homes[chunk]
        ref[row : row + CHUNK, cut] = value

    gate_half(
        other_half(), spread_ref, leaving_ref, query_ref, states_ref, before_ref,
        (one_ref, two_ref, three_ref), lambda cut: near_ref[:, cut], put,
    )


def keep_kernel(
    spread_ref, leaving_ref, query_ref, taps_ref, keys_ref, values_ref, states_ref, before_ref,
    one_ref, two_ref, three_ref, out_ref, turned_ref, near_ref,
):
    half = 1 - other_half()
    rows = near_ref.shape[0]

    def put_near(cut, value):
        near_ref[:, cut] = value

    def put(chunk, cut, value):
        out_ref[chunk * CHUNK : (chunk + 1) * CHUNK, cut] = value

    convolve_half(
        pl.multiple_of(half * rows, rows), taps_ref, keys_ref, values_ref, turned_ref, put_near
    )
    gate_half(
        half, spread_ref, leaving_ref, query_ref, states_ref, before_ref,
        (one_ref, two_ref, three_ref), lambda cut: near_ref[:, cut], put,
    )


def vmem():
    return pl.BlockSpec(memory_space=pltpu.VMEM)


def anywhere():
    return pl.BlockSpec(memory_space=pl.ANY)


def cost(us):
    return pl.CostEstimate(flops=0, transcendentals=0, bytes_accessed=int(us * 3.0e6))


def call(kernel, us, out_shape, *args, scratch=()):
    return pl.pallas_call(
        kernel,
        out_shape=out_shape,
        in_specs=[vmem()] * len(args),
        out_specs=jax.tree.map(lambda _: vmem(), out_shape),
        scratch_shapes=list(scratch),
        cost_estimate=cost(us),
        compiler_params=pltpu.CompilerParams(vmem_limit_bytes=LIMIT),
    )(*args)


def place():
    ctx = lax.axis_index("ctx")
    tp = lax.axis_index("tp")
    return {"y": ctx // 4, "far": ctx // 2 % 2, "core": ctx % 2, "near": tp // 4, "z": tp % 4}


def route(change):
    pairs = []
    for index in range(128):
        ctx, tp = divmod(index, 8)
        spot = {"y": ctx // 4, "far": ctx // 2 % 2, "core": ctx % 2, "near": tp // 4, "z": tp % 4}
        spot.update(change(spot))
        there = spot["y"] * 4 + spot["far"] * 2 + spot["core"]
        pairs.append((index, there * 8 + spot["near"] * 4 + spot["z"]))
    return pairs


def move(array, change):
    return lax.ppermute(array, ("ctx", "tp"), route(change))


def along(axis, size, by):
    return lambda spot: {axis: (spot[axis] + by) % size}


def either_side(spot):
    x = spot["far"] * 2 + spot["near"]
    step = 1 if x % 2 == spot["core"] else -1
    x = (x + step) % 4
    return {"far": x // 2, "near": x % 2}


def column_blocks(steps):
    tp = lax.axis_index("tp")
    near, z = tp // 4, tp % 4
    return [((1 - near) * 4 if other else near * 4) + ((z + step) & 3) for step, other in steps]


def gather_kernel(*refs):
    piece_refs, out_ref, sems = refs[:4], refs[4], refs[5]
    core = lax.axis_index("ctx") % 2
    copies = []
    for index, piece in enumerate(piece_refs):
        half = core if index < 2 else 1 - core
        row = pl.multiple_of(half * 256 + index % 2 * EARLY, 32)
        copies.append(
            pltpu.make_async_copy(piece, out_ref.at[pl.ds(row, piece.shape[0])], sems.at[index])
        )
        copies[-1].start()
    for copy in copies:
        copy.wait()


def gather(pieces):
    return pl.pallas_call(
        gather_kernel,
        out_shape=jax.ShapeDtypeStruct((512, pieces[0].shape[1]), jnp.bfloat16),
        in_specs=[anywhere()] * 4,
        out_specs=vmem(),
        scratch_shapes=[pltpu.SemaphoreType.DMA((4,))],
        cost_estimate=cost(2),
        compiler_params=pltpu.CompilerParams(vmem_limit_bytes=LIMIT),
    )(*pieces)


def project_kernel(steps, start, *refs):
    mine_ref, theirs_ref, own_ref, got_ref = refs[:4]
    out_refs = refs[4:]
    rows = theirs_ref.shape[0]
    mine = mine_ref[start : start + rows]
    theirs = theirs_ref[...]
    for out_ref, block in zip(out_refs, column_blocks(steps)):
        columns = pl.ds(pl.multiple_of(block * 512, 512), 512)
        total = jnp.dot(mine, own_ref[:, columns], preferred_element_type=jnp.float32)
        total += jnp.dot(theirs, got_ref[:, columns], preferred_element_type=jnp.float32)
        out_ref[...] = total.astype(jnp.bfloat16)


def project(steps, start, mine, theirs, own, got):
    count = len(steps)
    out = jax.ShapeDtypeStruct(theirs.shape, jnp.bfloat16)
    return call(
        functools.partial(project_kernel, steps, start), count, [out] * count, mine, theirs, own, got
    )


def finish_kernel(*refs):
    out_ref = refs[-1]
    near = lax.axis_index("tp") // 4
    start = 0
    for part, rows in enumerate(PARTS):
        own = refs[part]
        right, left, swapped = refs[len(PARTS) + part * 3 : len(PARTS) + part * 3 + 3]
        total = own[...].astype(jnp.float32) + right[...].astype(jnp.float32)
        total = (total + left[...].astype(jnp.float32)).astype(jnp.bfloat16)
        here = pl.multiple_of(near * sum(PARTS) + start, CHUNK)
        there = pl.multiple_of((1 - near) * sum(PARTS) + start, CHUNK)
        out_ref[pl.ds(here, rows), :] = total
        out_ref[pl.ds(there, rows), :] = swapped[...]
        start += rows


def plus(*arrays):
    total = arrays[0].astype(jnp.float32)
    for array in arrays[1:]:
        total = total + array.astype(jnp.float32)
    return total.astype(jnp.bfloat16)


def layer(query, keys, values, residues, rates, w_out):
    length, width = keys.shape
    spot = place()
    shape = jax.ShapeDtypeStruct

    slab = lax.dynamic_slice_in_dim(w_out, spot["core"] * 256, EARLY, 0)
    slab, rates = lax.optimization_barrier((slab, rates))
    early = move(slab, either_side)

    small = shape((STATE, width), jnp.float32)
    states, last, spread, leaving, taps, weights = pl.pallas_call(
        state_kernel,
        out_shape=(
            shape((length // CHUNK * STATE, width), jnp.float32),
            small,
            small,
            shape((CHUNK, width), jnp.bfloat16),
            shape((width // SHARE * CHUNK, CHUNK), jnp.bfloat16),
            shape((7 * STATE, width), jnp.float32),
        ),
        in_specs=[anywhere()] * 4,
        out_specs=[vmem()] * 6,
        scratch_shapes=[
            pltpu.VMEM(rates.T.shape, jnp.float32),
            pltpu.VMEM(rates.T.shape, jnp.float32),
            pltpu.VMEM(keys.shape, jnp.bfloat16),
            pltpu.VMEM(keys.shape, jnp.bfloat16),
            pltpu.SemaphoreType.DMA((4,)),
        ],
        cost_estimate=cost(3),
        compiler_params=pltpu.CompilerParams(vmem_limit_bytes=LIMIT),
    )(rates.T, residues.T, keys, values)
    last, core = lax.optimization_barrier((last, spot["core"]))
    slab = lax.dynamic_slice_in_dim(w_out, core * 256 + EARLY, 256 - EARLY, 0)
    near = []
    for k in range(1, 4):
        pairs = [(c, c // 4 * 4 + (c % 4 + k) % 4) for c in range(16)]
        near.append(lax.ppermute(last, "ctx", pairs))
    late = move(slab, either_side)
    weights = weights.reshape(7, STATE, width)
    total = last * weights[0] + near[0] * weights[1] + near[1] * weights[2] + near[2] * weights[3]
    before = near[0] * weights[4] + near[1] * weights[5] + near[2] * weights[6]
    above = [
        lax.ppermute(total, "ctx", [(c, c + 4 * k) for c in range(16 - 4 * k)])
        for k in range(1, 4)
    ]
    tall = shape((length // 2, width), jnp.bfloat16)
    turned = pltpu.VMEM((width // LANES, LANES, length // 2), jnp.bfloat16)
    local = call(near_kernel, 3, tall, taps, keys, values, scratch=[turned])
    above, local = lax.optimization_barrier((above, local))
    others = call(
        send_kernel, 2, [shape((rows, width), jnp.bfloat16) for rows in PARTS],
        spread, leaving, query, local, states, before, *above,
    )
    theirs = [move(other, along("near", 2, 1)) for other in others]
    mine = call(
        keep_kernel, 4, tall,
        spread, leaving, query, taps, keys, values, states, before, *above,
        scratch=[turned, pltpu.VMEM((length // 2, width), jnp.bfloat16)],
    )
    early, late, others = lax.optimization_barrier((early, late, others))
    got = gather([early, late, move(early, along("core", 2, 1)), move(late, along("core", 2, 1))])

    finals, rest = [], []
    for part in range(len(PARTS)):
        start = sum(PARTS[:part])
        if part:
            theirs[part], finals = lax.optimization_barrier((theirs[part], finals))
        args = (start, mine, theirs[part], w_out, got)
        far_p, far_o = project(((2, True), (2, False)), *args)
        right_o, left_p, right_p, left_o, own_p, own_o = project(
            ((1, False), (-1, True), (1, True), (-1, False), (0, True), (0, False)), *args
        )
        finals.append(own_o)
        far_p = move(far_p, along("z", 4, 1))
        far_o = move(far_o, along("z", 4, -1))
        right_o = move(right_o, along("z", 4, 1))
        left_p = move(left_p, along("z", 4, -1))
        right_p = move(plus(right_p, far_p), along("z", 4, 1))
        left_o = move(plus(left_o, far_o), along("z", 4, -1))
        swapped = move(plus(own_p, right_p, left_p), along("near", 2, 1))
        rest += [right_o, left_o, swapped]
    return call(finish_kernel, 1, shape((length, 512), jnp.bfloat16), *finals, *rest)


def solution(mesh):
    in_specs = (P("ctx", "tp"), P("ctx", "tp"), P("ctx", "tp"), P(), P(), P("tp", None))
    return jax.shard_map(
        layer, mesh=mesh, in_specs=in_specs, out_specs=P("ctx", "tp"), check_vma=False
    )
```

```python
import functools
import jax
import jax.numpy as jnp
from jax import lax
from jax.experimental import pallas as pl
from jax.experimental.pallas import tpu as pltpu
from jax.sharding import PartitionSpec as P


SHARE = 16
STATE = 16
CHUNK = 128
PARTS = (128, 256, 128)
SHARED = 64
LIMIT = 12 * 2**20
SPAN = 1024
LANES = 128
PACK = LANES // SHARE


def as_row(spread):
    state = lax.broadcasted_iota(jnp.int32, spread.shape, 0)
    slot = lax.broadcasted_iota(jnp.int32, spread.shape, 1) % STATE
    return jnp.sum(jnp.where(state == slot, spread, 0.0), axis=0, keepdims=True)


def same_group():
    left = lax.broadcasted_iota(jnp.int32, (LANES, LANES), 0) // STATE
    right = lax.broadcasted_iota(jnp.int32, (LANES, LANES), 1) // SHARE
    return left == right


def spread_modes(modes, width):
    groups = modes.shape[1]
    first = lax.axis_index("tp") * (width // SHARE)
    group = lax.broadcasted_iota(jnp.int32, (groups, width), 0) - first
    owner = lax.broadcasted_iota(jnp.int32, (groups, width), 1) // SHARE
    return exact_dot(modes, (group == owner).astype(jnp.float32), 0)


def exact_dot(left, right, side):
    return lax.dot_general(
        left, right, (((1,), (side,)), ((), ())),
        precision=lax.Precision.HIGHEST, preferred_element_type=jnp.float32,
    )


def as_column(modes, width):
    groups = modes.shape[1]
    first = lax.axis_index("tp") * (width // SHARE)
    group = lax.broadcasted_iota(jnp.int32, (width, groups), 1) - first
    owner = lax.broadcasted_iota(jnp.int32, (width, groups), 0) // STATE
    wide = exact_dot((group == owner).astype(jnp.float32), modes, 1)
    slot = lax.broadcasted_iota(jnp.int32, wide.shape, 0) % STATE
    state = lax.broadcasted_iota(jnp.int32, wide.shape, 1)
    return jnp.sum(jnp.where(state == slot, wide, 0.0), axis=1, keepdims=True)


def state_kernel(
    modes_ref, keys_ref, values_ref,
    states_ref, last_ref, spread_ref, leaving_ref, taps_ref, product_ref,
):
    length, width = keys_ref.shape
    chunks = length // CHUNK
    rates = modes_ref[:STATE]
    spread = spread_modes(rates, width)
    spread_ref[...] = spread
    column = as_column(rates, width)
    step = jnp.exp(-float(CHUNK) * spread)
    ahead = (CHUNK - 1 - lax.broadcasted_iota(jnp.int32, (LANES, CHUNK), 1)).astype(jnp.float32)
    keep = same_group()
    gains = modes_ref[STATE:] * jnp.sqrt(2.0 * rates)
    rate_row = as_row(spread)
    gain_row = as_row(spread_modes(gains, width))
    after = (1 + lax.broadcasted_iota(jnp.int32, (CHUNK, width), 0)).astype(jnp.float32)
    leaving_ref[...] = (gain_row * jnp.exp(-rate_row * after)).astype(jnp.bfloat16)
    fadings = []
    for block in range(width // LANES):
        cut = slice(block * LANES, (block + 1) * LANES)
        fading = jnp.exp(-column[cut] * ahead)
        fadings.append(fading)
        fading = fading.astype(jnp.bfloat16)
        decay = step[:, cut]
        carried = jnp.zeros((STATE, LANES), jnp.float32)
        for chunk in range(chunks):
            rows = slice(chunk * CHUNK, (chunk + 1) * CHUNK)
            product = (
                keys_ref[rows, cut].astype(jnp.float32) * values_ref[rows, cut].astype(jnp.float32)
            ).astype(jnp.bfloat16)
            product_ref[rows, cut] = product
            full = jnp.dot(fading, product, preferred_element_type=jnp.float32)
            state = jnp.sum(jnp.where(keep, full, 0.0).reshape(PACK, STATE, LANES), axis=0)
            states_ref[chunk * STATE : (chunk + 1) * STATE, cut] = state
            carried = carried * decay + state
        last_ref[:, cut] = carried
    causal = lax.broadcasted_iota(jnp.int32, (CHUNK, CHUNK), 0) >= lax.broadcasted_iota(
        jnp.int32, (CHUNK, CHUNK), 1
    )
    for block in range(width // LANES):
        cut = slice(block * LANES, (block + 1) * LANES)
        entering = (fadings[block] * jnp.exp(column[cut] * float(CHUNK))).astype(jnp.bfloat16)
        leaving = leaving_ref[:, cut]
        for group in range(PACK):
            at = group * SHARE
            rows = [entering[at : at + SHARE]]
            if group:
                rows.insert(0, jnp.zeros((at, CHUNK), jnp.bfloat16))
            if group < PACK - 1:
                rows.append(jnp.zeros((LANES - at - SHARE, CHUNK), jnp.bfloat16))
            taps = jnp.dot(
                leaving, jnp.concatenate(rows, axis=0), preferred_element_type=jnp.float32
            )
            index = block * PACK + group
            taps_ref[index * CHUNK : (index + 1) * CHUNK, :] = jnp.where(causal, taps, 0.0).astype(
                jnp.bfloat16
            )


def join_kernel(spread_ref, last_ref, one_ref, two_ref, three_ref, total_ref, before_ref, again_ref):
    span = float(SPAN)
    spread = spread_ref[...]
    again_ref[...] = spread
    mine = lax.axis_index("ctx") % 4
    total = last_ref[...] * jnp.exp(-span * (3 - mine).astype(jnp.float32) * spread)
    before = jnp.zeros_like(total)
    for k, ref in ((1, one_ref), (2, two_ref), (3, three_ref)):
        near = ref[...]
        source = mine ^ k
        total = total + near * jnp.exp(-span * (3 - source).astype(jnp.float32) * spread)
        gap = jnp.maximum(mine - source - 1, 0).astype(jnp.float32)
        before = before + jnp.where(mine > source, near * jnp.exp(-span * gap * spread), 0.0)
    total_ref[...] = total
    before_ref[...] = before


def convolve_half(start, taps_ref, product_ref, turned_ref, put):
    rows = product_ref.shape[0] // 2
    chunks = rows // CHUNK
    for block in range(product_ref.shape[1] // LANES):
        cut = slice(block * LANES, (block + 1) * LANES)
        turned = product_ref[pl.ds(start, rows), cut].T
        for group in range(PACK):
            at = group * SHARE
            index = block * PACK + group
            stacked = jnp.concatenate(
                [turned[at : at + SHARE, c * CHUNK : (c + 1) * CHUNK] for c in range(chunks)], axis=0
            )
            folded = lax.dot_general(
                stacked,
                taps_ref[index * CHUNK : (index + 1) * CHUNK, :],
                (((1,), (1,)), ((), ())),
                preferred_element_type=jnp.float32,
            ).astype(jnp.bfloat16)
            for c in range(chunks):
                turned_ref[block, at : at + SHARE, c * CHUNK : (c + 1) * CHUNK] = (
                    folded[c * SHARE : (c + 1) * SHARE]
                )
        put(cut, turned_ref[block].T)


def gate_half(
    half, spread_ref, leaving_ref, query_ref, states_ref, before_ref, above_refs, local, put
):
    length, width = query_ref.shape
    chunks = length // CHUNK // 2
    span = float(SPAN)
    mine = lax.axis_index("ctx") % 4
    spread = spread_ref[...]
    step = jnp.exp(-float(CHUNK) * spread)
    group_step = jnp.exp(-4.0 * span * spread)
    one, two, three = [ref[...] for ref in above_refs]
    above = one + group_step * (two + group_step * three)
    entry = before_ref[...] + above * jnp.exp(-span * mine.astype(jnp.float32) * spread)
    keep = same_group()
    moved = entry
    for chunk in range(chunks):
        moved = moved * step + states_ref[chunk * STATE : (chunk + 1) * STATE, :]
    entry = jnp.where(half == 1, moved, entry)
    start = pl.multiple_of(half * (length // 2), length // 2)
    states = states_ref[pl.ds(pl.multiple_of(half * chunks * STATE, chunks * STATE), chunks * STATE), :]
    for block in range(width // LANES):
        cut = slice(block * LANES, (block + 1) * LANES)
        leaving = leaving_ref[:, cut]
        carried = entry[:, cut]
        near = local(cut)
        query = query_ref[pl.ds(start, length // 2), cut]
        for chunk in range(chunks):
            rows = slice(chunk * CHUNK, (chunk + 1) * CHUNK)
            tall = jnp.concatenate([carried] * PACK, axis=0)
            tall = jnp.where(keep, tall, 0.0).astype(jnp.bfloat16)
            earlier = jnp.dot(leaving, tall, preferred_element_type=jnp.float32)
            convolved = (near[rows].astype(jnp.float32) + earlier).astype(jnp.bfloat16)
            gated = query[rows].astype(jnp.float32) * convolved.astype(jnp.float32)
            put(chunk, cut, gated.astype(jnp.bfloat16))
            carried = carried * step[:, cut] + states[chunk * STATE : (chunk + 1) * STATE, cut]


def other_half():
    return 1 - lax.axis_index("tp") // 4


def near_kernel(taps_ref, product_ref, out_ref, turned_ref):
    rows = out_ref.shape[0]
    start = pl.multiple_of(other_half() * rows, rows)

    def put(cut, value):
        out_ref[:, cut] = value

    convolve_half(start, taps_ref, product_ref, turned_ref, put)


def send_kernel(
    spread_ref, leaving_ref, query_ref, near_ref, states_ref, before_ref,
    one_ref, two_ref, three_ref, *out_refs,
):
    homes = [(ref, row) for ref in out_refs for row in range(0, ref.shape[0], CHUNK)]

    def put(chunk, cut, value):
        ref, row = homes[chunk]
        ref[row : row + CHUNK, cut] = value

    gate_half(
        other_half(), spread_ref, leaving_ref, query_ref, states_ref, before_ref,
        (one_ref, two_ref, three_ref), lambda cut: near_ref[:, cut], put,
    )


def keep_kernel(
    spread_ref, leaving_ref, query_ref, taps_ref, product_ref, states_ref, before_ref,
    one_ref, two_ref, three_ref, out_ref, turned_ref, near_ref,
):
    half = 1 - other_half()
    rows = near_ref.shape[0]

    def put_near(cut, value):
        near_ref[:, cut] = value

    def put(chunk, cut, value):
        out_ref[chunk * CHUNK : (chunk + 1) * CHUNK, cut] = value

    convolve_half(
        pl.multiple_of(half * rows, rows), taps_ref, product_ref, turned_ref, put_near
    )
    gate_half(
        half, spread_ref, leaving_ref, query_ref, states_ref, before_ref,
        (one_ref, two_ref, three_ref), lambda cut: near_ref[:, cut], put,
    )


def vmem():
    return pl.BlockSpec(memory_space=pltpu.VMEM)


def anywhere():
    return pl.BlockSpec(memory_space=pl.ANY)


def cost(us):
    return pl.CostEstimate(flops=0, transcendentals=0, bytes_accessed=int(us * 3.0e6))


def call(kernel, us, out_shape, *args, scratch=()):
    return pl.pallas_call(
        kernel,
        out_shape=out_shape,
        in_specs=[vmem()] * len(args),
        out_specs=jax.tree.map(lambda _: vmem(), out_shape),
        scratch_shapes=list(scratch),
        cost_estimate=cost(us),
        compiler_params=pltpu.CompilerParams(vmem_limit_bytes=LIMIT),
    )(*args)


def route(change):
    pairs = []
    for index in range(128):
        ctx, tp = divmod(index, 8)
        spot = {"y": ctx // 4, "far": ctx // 2 % 2, "core": ctx % 2, "near": tp // 4, "z": tp % 4}
        spot.update(change(spot))
        there = spot["y"] * 4 + spot["far"] * 2 + spot["core"]
        pairs.append((index, there * 8 + spot["near"] * 4 + spot["z"]))
    return pairs


def move(array, change):
    return lax.ppermute(array, ("ctx", "tp"), route(change))


def along(axis, size, by):
    return lambda spot: {axis: (spot[axis] + by) % size}


def either_side(spot):
    x = spot["far"] * 2 + spot["near"]
    step = 1 if x % 2 == spot["core"] else -1
    x = (x + step) % 4
    return {"far": x // 2, "near": x % 2}


def column_blocks(steps):
    tp = lax.axis_index("tp")
    near, z = tp // 4, tp % 4
    return [((1 - near) * 4 if other else near * 4) + ((z + step) & 3) for step, other in steps]


def slab_kernel(w_ref, shared_ref, common_ref, sems):
    ctx = lax.axis_index("ctx")
    row = pl.multiple_of(ctx % 2 * 256, 256)
    odd = pl.multiple_of(row + ctx // 4 % 2 * SHARED, SHARED)
    common = common_ref.shape[0]
    copies = [
        pltpu.make_async_copy(w_ref.at[pl.ds(odd, SHARED)], shared_ref, sems.at[0]),
        pltpu.make_async_copy(w_ref.at[pl.ds(row + 2 * SHARED, common)], common_ref, sems.at[1]),
    ]
    for copy in copies:
        copy.start()
    for copy in copies:
        copy.wait()


def cut_slabs(w_out):
    return pl.pallas_call(
        slab_kernel,
        out_shape=[
            jax.ShapeDtypeStruct((rows, w_out.shape[1]), w_out.dtype)
            for rows in (SHARED, 256 - 2 * SHARED)
        ],
        in_specs=[anywhere()],
        out_specs=[vmem()] * 2,
        scratch_shapes=[pltpu.SemaphoreType.DMA((2,))],
        cost_estimate=cost(1),
        compiler_params=pltpu.CompilerParams(vmem_limit_bytes=60 * 2**20),
    )(w_out)


def gather_kernel(*refs):
    piece_refs, out_ref, sems = refs[:-2], refs[-2], refs[-1]
    ctx = lax.axis_index("ctx")
    core, odd = ctx % 2, ctx // 4 % 2
    offsets = (odd * SHARED, (1 - odd) * SHARED, (1 - odd) * SHARED + SHARED // 2, 2 * SHARED)
    copies = []
    for index, piece in enumerate(piece_refs):
        half = core if index < 4 else 1 - core
        row = pl.multiple_of(half * 256 + offsets[index % 4], SHARED // 2)
        copies.append(
            pltpu.make_async_copy(piece, out_ref.at[pl.ds(row, piece.shape[0])], sems.at[index])
        )
        copies[-1].start()
    for copy in copies:
        copy.wait()


def gather(pieces):
    return pl.pallas_call(
        gather_kernel,
        out_shape=jax.ShapeDtypeStruct((512, pieces[0].shape[1]), jnp.bfloat16),
        in_specs=[anywhere()] * len(pieces),
        out_specs=vmem(),
        scratch_shapes=[pltpu.SemaphoreType.DMA((len(pieces),))],
        cost_estimate=cost(2),
        compiler_params=pltpu.CompilerParams(vmem_limit_bytes=LIMIT),
    )(*pieces)


def project_kernel(steps, start, *refs):
    mine_ref, theirs_ref, own_ref, got_ref = refs[:4]
    out_refs = refs[4:]
    rows = theirs_ref.shape[0]
    mine = mine_ref[start : start + rows]
    theirs = theirs_ref[...]
    for out_ref, block in zip(out_refs, column_blocks(steps)):
        columns = pl.ds(pl.multiple_of(block * 512, 512), 512)
        total = jnp.dot(mine, own_ref[:, columns], preferred_element_type=jnp.float32)
        total += jnp.dot(theirs, got_ref[:, columns], preferred_element_type=jnp.float32)
        out_ref[...] = total.astype(jnp.bfloat16)


def project(steps, start, mine, theirs, own, got):
    count = len(steps)
    out = jax.ShapeDtypeStruct(theirs.shape, jnp.bfloat16)
    return call(
        functools.partial(project_kernel, steps, start), count, [out] * count, mine, theirs, own, got
    )


def finish_kernel(*refs):
    out_ref = refs[-1]
    near = lax.axis_index("tp") // 4
    start = 0
    for part, rows in enumerate(PARTS):
        own = refs[part]
        right, left, swapped = refs[len(PARTS) + part * 3 : len(PARTS) + part * 3 + 3]
        total = own[...].astype(jnp.float32) + right[...].astype(jnp.float32)
        total = (total + left[...].astype(jnp.float32)).astype(jnp.bfloat16)
        here = pl.multiple_of(near * sum(PARTS) + start, CHUNK)
        there = pl.multiple_of((1 - near) * sum(PARTS) + start, CHUNK)
        out_ref[pl.ds(here, rows), :] = total
        out_ref[pl.ds(there, rows), :] = swapped[...]
        start += rows


def plus(*arrays):
    total = arrays[0].astype(jnp.float32)
    for array in arrays[1:]:
        total = total + array.astype(jnp.float32)
    return total.astype(jnp.bfloat16)


def layer(query, keys, values, residues, rates, w_out):
    length, width = keys.shape
    shape = jax.ShapeDtypeStruct

    modes = jnp.concatenate([rates.T, residues.T])
    shared, common = cut_slabs(w_out)
    shared = move(shared, either_side)
    common = move(common, either_side)
    fetched = [
        shared,
        move(shared[: SHARED // 2], along("y", 4, 1)),
        move(shared[SHARED // 2 :], along("y", 4, -1)),
        common,
    ]

    small = shape((STATE, width), jnp.float32)
    states, last, spread, leaving, taps, product = call(
        state_kernel,
        3,
        (
            shape((length // CHUNK * STATE, width), jnp.float32),
            small,
            small,
            shape((CHUNK, width), jnp.bfloat16),
            shape((width // SHARE * CHUNK, CHUNK), jnp.bfloat16),
            shape(keys.shape, jnp.bfloat16),
        ),
        modes, keys, values,
    )
    near = []
    for k in range(1, 4):
        pairs = [(c, c ^ k) for c in range(16)]
        near.append(lax.ppermute(last, "ctx", pairs))
    total, before, spread = call(join_kernel, 1, (small, small, small), spread, last, *near)
    above = [
        lax.ppermute(total, "ctx", [(c, c + 4 * k) for c in range(16 - 4 * k)])
        for k in range(1, 4)
    ]
    tall = shape((length // 2, width), jnp.bfloat16)
    turned = pltpu.VMEM((width // LANES, LANES, length // 2), jnp.bfloat16)
    local = call(near_kernel, 3, tall, taps, product, scratch=[turned])
    above, local = lax.optimization_barrier((above, local))
    others = call(
        send_kernel, 2, [shape((rows, width), jnp.bfloat16) for rows in PARTS],
        spread, leaving, query, local, states, before, *above,
    )
    theirs = [move(other, along("near", 2, 1)) for other in others]
    mine = call(
        keep_kernel, 4, tall,
        spread, leaving, query, taps, product, states, before, *above,
        scratch=[turned, pltpu.VMEM((length // 2, width), jnp.bfloat16)],
    )
    common, others = lax.optimization_barrier((common, others))
    fetched[3] = common
    swapped = [move(piece, along("core", 2, 1)) for piece in fetched]
    pieces = fetched + swapped
    got = gather(pieces)

    finals, rest = [], []
    for part in range(len(PARTS)):
        start = sum(PARTS[:part])
        if part:
            theirs[part], free = lax.optimization_barrier((theirs[part], free))
        args = (start, mine, theirs[part], w_out, got)
        far = ((2, True), (2, False))
        near_free = ((1, False), (-1, True))
        rest_steps = ((1, True), (-1, False), (0, True), (0, False))
        first = far if part else far + near_free
        last_ones = near_free + rest_steps if part else rest_steps
        blocks = project(first, *args)
        blocks += project(last_ones, *args)
        far_p, far_o, right_o, left_p, right_p, left_o, own_p, own_o = blocks
        finals.append(own_o)
        free = right_o
        far_p = move(far_p, along("z", 4, 1))
        far_o = move(far_o, along("z", 4, -1))
        right_o = move(right_o, along("z", 4, 1))
        left_p = move(left_p, along("z", 4, -1))
        right_p = move(plus(right_p, far_p), along("z", 4, 1))
        left_o = move(plus(left_o, far_o), along("z", 4, -1))
        swapped = move(plus(own_p, right_p, left_p), along("near", 2, 1))
        rest += [right_o, left_o, swapped]
    return call(finish_kernel, 1, shape((length, 512), jnp.bfloat16), *finals, *rest)


def solution(mesh):
    in_specs = (P("ctx", "tp"), P("ctx", "tp"), P("ctx", "tp"), P(), P(), P("tp", None))
    return jax.shard_map(
        layer, mesh=mesh, in_specs=in_specs, out_specs=P("ctx", "tp"), check_vma=False
    )
```

```python
import functools
import jax
import jax.numpy as jnp
from jax import lax
from jax.experimental import pallas as pl
from jax.experimental.pallas import tpu as pltpu
from jax.sharding import PartitionSpec as P


SHARE = 16
STATE = 16
CHUNK = 128
PARTS = (128, 256, 128)
SHARED = 64
LIMIT = 12 * 2**20
SPAN = 1024
LANES = 128
PACK = LANES // SHARE


def as_row(spread):
    state = lax.broadcasted_iota(jnp.int32, spread.shape, 0)
    slot = lax.broadcasted_iota(jnp.int32, spread.shape, 1) % STATE
    return jnp.sum(jnp.where(state == slot, spread, 0.0), axis=0, keepdims=True)


def same_group():
    left = lax.broadcasted_iota(jnp.int32, (LANES, LANES), 0) // STATE
    right = lax.broadcasted_iota(jnp.int32, (LANES, LANES), 1) // SHARE
    return left == right


def spread_modes(modes, width):
    groups = modes.shape[1]
    first = lax.axis_index("tp") * (width // SHARE)
    group = lax.broadcasted_iota(jnp.int32, (groups, width), 0) - first
    owner = lax.broadcasted_iota(jnp.int32, (groups, width), 1) // SHARE
    return exact_dot(modes, (group == owner).astype(jnp.float32), 0)


def exact_dot(left, right, side):
    return lax.dot_general(
        left, right, (((1,), (side,)), ((), ())),
        precision=lax.Precision.HIGHEST, preferred_element_type=jnp.float32,
    )


def as_column(modes, width):
    groups = modes.shape[1]
    first = lax.axis_index("tp") * (width // SHARE)
    group = lax.broadcasted_iota(jnp.int32, (width, groups), 1) - first
    owner = lax.broadcasted_iota(jnp.int32, (width, groups), 0) // STATE
    wide = exact_dot((group == owner).astype(jnp.float32), modes, 1)
    slot = lax.broadcasted_iota(jnp.int32, wide.shape, 0) % STATE
    state = lax.broadcasted_iota(jnp.int32, wide.shape, 1)
    return jnp.sum(jnp.where(state == slot, wide, 0.0), axis=1, keepdims=True)


def state_kernel(
    modes_ref, keys_ref, values_ref,
    states_ref, last_ref, spread_ref, leaving_ref, taps_ref, product_ref,
):
    length, width = keys_ref.shape
    chunks = length // CHUNK
    rates = modes_ref[:STATE]
    spread = spread_modes(rates, width)
    spread_ref[...] = spread
    column = as_column(rates, width)
    step = jnp.exp(-float(CHUNK) * spread)
    ahead = (CHUNK - 1 - lax.broadcasted_iota(jnp.int32, (LANES, CHUNK), 1)).astype(jnp.float32)
    keep = same_group()
    gains = modes_ref[STATE:] * jnp.sqrt(2.0 * rates)
    rate_row = as_row(spread)
    gain_row = as_row(spread_modes(gains, width))
    after = (1 + lax.broadcasted_iota(jnp.int32, (CHUNK, width), 0)).astype(jnp.float32)
    leaving_ref[...] = (gain_row * jnp.exp(-rate_row * after)).astype(jnp.bfloat16)
    fadings = []
    for block in range(width // LANES):
        cut = slice(block * LANES, (block + 1) * LANES)
        fading = jnp.exp(-column[cut] * ahead)
        fadings.append(fading)
        fading = fading.astype(jnp.bfloat16)
        decay = step[:, cut]
        carried = jnp.zeros((STATE, LANES), jnp.float32)
        for chunk in range(chunks):
            rows = slice(chunk * CHUNK, (chunk + 1) * CHUNK)
            product = (
                keys_ref[rows, cut].astype(jnp.float32) * values_ref[rows, cut].astype(jnp.float32)
            ).astype(jnp.bfloat16)
            product_ref[rows, cut] = product
            full = jnp.dot(fading, product, preferred_element_type=jnp.float32)
            state = jnp.sum(jnp.where(keep, full, 0.0).reshape(PACK, STATE, LANES), axis=0)
            states_ref[chunk * STATE : (chunk + 1) * STATE, cut] = state
            carried = carried * decay + state
        last_ref[:, cut] = carried
    causal = lax.broadcasted_iota(jnp.int32, (CHUNK, CHUNK), 0) >= lax.broadcasted_iota(
        jnp.int32, (CHUNK, CHUNK), 1
    )
    for block in range(width // LANES):
        cut = slice(block * LANES, (block + 1) * LANES)
        entering = (fadings[block] * jnp.exp(column[cut] * float(CHUNK))).astype(jnp.bfloat16)
        leaving = leaving_ref[:, cut]
        for group in range(PACK):
            at = group * SHARE
            rows = [entering[at : at + SHARE]]
            if group:
                rows.insert(0, jnp.zeros((at, CHUNK), jnp.bfloat16))
            if group < PACK - 1:
                rows.append(jnp.zeros((LANES - at - SHARE, CHUNK), jnp.bfloat16))
            taps = jnp.dot(
                leaving, jnp.concatenate(rows, axis=0), preferred_element_type=jnp.float32
            )
            index = block * PACK + group
            taps_ref[index * CHUNK : (index + 1) * CHUNK, :] = jnp.where(causal, taps, 0.0).astype(
                jnp.bfloat16
            )


def join_kernel(spread_ref, last_ref, one_ref, two_ref, three_ref, total_ref, before_ref, again_ref):
    span = float(SPAN)
    spread = spread_ref[...]
    again_ref[...] = spread
    mine = lax.axis_index("ctx") % 4
    total = last_ref[...] * jnp.exp(-span * (3 - mine).astype(jnp.float32) * spread)
    before = jnp.zeros_like(total)
    for k, ref in ((1, one_ref), (2, two_ref), (3, three_ref)):
        near = ref[...]
        source = mine ^ k
        total = total + near * jnp.exp(-span * (3 - source).astype(jnp.float32) * spread)
        gap = jnp.maximum(mine - source - 1, 0).astype(jnp.float32)
        before = before + jnp.where(mine > source, near * jnp.exp(-span * gap * spread), 0.0)
    total_ref[...] = total
    before_ref[...] = before


def convolve_half(start, taps_ref, product_ref, turned_ref, put):
    rows = product_ref.shape[0] // 2
    chunks = rows // CHUNK
    for block in range(product_ref.shape[1] // LANES):
        cut = slice(block * LANES, (block + 1) * LANES)
        turned = product_ref[pl.ds(start, rows), cut].T
        for group in range(PACK):
            at = group * SHARE
            index = block * PACK + group
            stacked = jnp.concatenate(
                [turned[at : at + SHARE, c * CHUNK : (c + 1) * CHUNK] for c in range(chunks)], axis=0
            )
            folded = lax.dot_general(
                stacked,
                taps_ref[index * CHUNK : (index + 1) * CHUNK, :],
                (((1,), (1,)), ((), ())),
                preferred_element_type=jnp.float32,
            ).astype(jnp.bfloat16)
            for c in range(chunks):
                turned_ref[block, at : at + SHARE, c * CHUNK : (c + 1) * CHUNK] = (
                    folded[c * SHARE : (c + 1) * SHARE]
                )
        put(cut, turned_ref[block].T)


def gate_half(
    half, spread_ref, leaving_ref, query_ref, states_ref, before_ref, above_refs, local, put
):
    length, width = query_ref.shape
    chunks = length // CHUNK // 2
    span = float(SPAN)
    mine = lax.axis_index("ctx") % 4
    spread = spread_ref[...]
    step = jnp.exp(-float(CHUNK) * spread)
    group_step = jnp.exp(-4.0 * span * spread)
    one, two, three = [ref[...] for ref in above_refs]
    above = one + group_step * (two + group_step * three)
    entry = before_ref[...] + above * jnp.exp(-span * mine.astype(jnp.float32) * spread)
    keep = same_group()
    moved = entry
    for chunk in range(chunks):
        moved = moved * step + states_ref[chunk * STATE : (chunk + 1) * STATE, :]
    entry = jnp.where(half == 1, moved, entry)
    start = pl.multiple_of(half * (length // 2), length // 2)
    states = states_ref[pl.ds(pl.multiple_of(half * chunks * STATE, chunks * STATE), chunks * STATE), :]
    for block in range(width // LANES):
        cut = slice(block * LANES, (block + 1) * LANES)
        leaving = leaving_ref[:, cut]
        carried = entry[:, cut]
        near = local(cut)
        query = query_ref[pl.ds(start, length // 2), cut]
        for chunk in range(chunks):
            rows = slice(chunk * CHUNK, (chunk + 1) * CHUNK)
            tall = jnp.concatenate([carried] * PACK, axis=0)
            tall = jnp.where(keep, tall, 0.0).astype(jnp.bfloat16)
            earlier = jnp.dot(leaving, tall, preferred_element_type=jnp.float32)
            convolved = (near[rows].astype(jnp.float32) + earlier).astype(jnp.bfloat16)
            gated = query[rows].astype(jnp.float32) * convolved.astype(jnp.float32)
            put(chunk, cut, gated.astype(jnp.bfloat16))
            carried = carried * step[:, cut] + states[chunk * STATE : (chunk + 1) * STATE, cut]


def other_half():
    return 1 - lax.axis_index("tp") // 4


def near_kernel(taps_ref, product_ref, out_ref, turned_ref):
    rows = out_ref.shape[0]
    start = pl.multiple_of(other_half() * rows, rows)

    def put(cut, value):
        out_ref[:, cut] = value

    convolve_half(start, taps_ref, product_ref, turned_ref, put)


def send_kernel(
    spread_ref, leaving_ref, query_ref, near_ref, states_ref, before_ref,
    one_ref, two_ref, three_ref, *out_refs,
):
    homes = [(ref, row) for ref in out_refs for row in range(0, ref.shape[0], CHUNK)]

    def put(chunk, cut, value):
        ref, row = homes[chunk]
        ref[row : row + CHUNK, cut] = value

    gate_half(
        other_half(), spread_ref, leaving_ref, query_ref, states_ref, before_ref,
        (one_ref, two_ref, three_ref), lambda cut: near_ref[:, cut], put,
    )


def keep_kernel(
    spread_ref, leaving_ref, query_ref, taps_ref, product_ref, states_ref, before_ref,
    one_ref, two_ref, three_ref, out_ref, turned_ref, near_ref,
):
    half = 1 - other_half()
    rows = near_ref.shape[0]

    def put_near(cut, value):
        near_ref[:, cut] = value

    def put(chunk, cut, value):
        out_ref[chunk * CHUNK : (chunk + 1) * CHUNK, cut] = value

    convolve_half(
        pl.multiple_of(half * rows, rows), taps_ref, product_ref, turned_ref, put_near
    )
    gate_half(
        half, spread_ref, leaving_ref, query_ref, states_ref, before_ref,
        (one_ref, two_ref, three_ref), lambda cut: near_ref[:, cut], put,
    )


def vmem():
    return pl.BlockSpec(memory_space=pltpu.VMEM)


def anywhere():
    return pl.BlockSpec(memory_space=pl.ANY)


def cost(us):
    return pl.CostEstimate(flops=0, transcendentals=0, bytes_accessed=int(us * 3.0e6))


def call(kernel, us, out_shape, *args, scratch=()):
    return pl.pallas_call(
        kernel,
        out_shape=out_shape,
        in_specs=[vmem()] * len(args),
        out_specs=jax.tree.map(lambda _: vmem(), out_shape),
        scratch_shapes=list(scratch),
        cost_estimate=cost(us),
        compiler_params=pltpu.CompilerParams(vmem_limit_bytes=LIMIT),
    )(*args)


def route(change):
    pairs = []
    for index in range(128):
        ctx, tp = divmod(index, 8)
        spot = {"y": ctx // 4, "far": ctx // 2 % 2, "core": ctx % 2, "near": tp // 4, "z": tp % 4}
        spot.update(change(spot))
        there = spot["y"] * 4 + spot["far"] * 2 + spot["core"]
        pairs.append((index, there * 8 + spot["near"] * 4 + spot["z"]))
    return pairs


def move(array, change):
    return lax.ppermute(array, ("ctx", "tp"), route(change))


def along(axis, size, by):
    return lambda spot: {axis: (spot[axis] + by) % size}


def either_side(spot):
    x = spot["far"] * 2 + spot["near"]
    step = 1 if x % 2 == spot["core"] else -1
    x = (x + step) % 4
    return {"far": x // 2, "near": x % 2}


def column_blocks(steps):
    tp = lax.axis_index("tp")
    near, z = tp // 4, tp % 4
    return [((1 - near) * 4 if other else near * 4) + ((z + step) & 3) for step, other in steps]


def slab_kernel(w_ref, shared_ref, common_ref, sems):
    ctx = lax.axis_index("ctx")
    row = pl.multiple_of(ctx % 2 * 256, 256)
    odd = pl.multiple_of(row + ctx // 4 % 2 * SHARED, SHARED)
    common = common_ref.shape[0]
    copies = [
        pltpu.make_async_copy(w_ref.at[pl.ds(odd, SHARED)], shared_ref, sems.at[0]),
        pltpu.make_async_copy(w_ref.at[pl.ds(row + 2 * SHARED, common)], common_ref, sems.at[1]),
    ]
    for copy in copies:
        copy.start()
    for copy in copies:
        copy.wait()


def cut_slabs(w_out):
    return pl.pallas_call(
        slab_kernel,
        out_shape=[
            jax.ShapeDtypeStruct((rows, w_out.shape[1]), w_out.dtype)
            for rows in (SHARED, 256 - 2 * SHARED)
        ],
        in_specs=[anywhere()],
        out_specs=[vmem()] * 2,
        scratch_shapes=[pltpu.SemaphoreType.DMA((2,))],
        cost_estimate=cost(1),
        compiler_params=pltpu.CompilerParams(vmem_limit_bytes=60 * 2**20),
    )(w_out)


def gather_kernel(*refs):
    piece_refs, out_ref, sems = refs[:-2], refs[-2], refs[-1]
    ctx = lax.axis_index("ctx")
    core, odd = ctx % 2, ctx // 4 % 2
    offsets = (odd * SHARED, (1 - odd) * SHARED, (1 - odd) * SHARED + SHARED // 2, 2 * SHARED)
    copies = []
    for index, piece in enumerate(piece_refs):
        half = core if index < 4 else 1 - core
        row = pl.multiple_of(half * 256 + offsets[index % 4], SHARED // 2)
        copies.append(
            pltpu.make_async_copy(piece, out_ref.at[pl.ds(row, piece.shape[0])], sems.at[index])
        )
        copies[-1].start()
    for copy in copies:
        copy.wait()


def gather(pieces):
    return pl.pallas_call(
        gather_kernel,
        out_shape=jax.ShapeDtypeStruct((512, pieces[0].shape[1]), jnp.bfloat16),
        in_specs=[anywhere()] * len(pieces),
        out_specs=vmem(),
        scratch_shapes=[pltpu.SemaphoreType.DMA((len(pieces),))],
        cost_estimate=cost(2),
        compiler_params=pltpu.CompilerParams(vmem_limit_bytes=LIMIT),
    )(*pieces)


def project_kernel(steps, start, *refs):
    mine_ref, theirs_ref, own_ref, got_ref = refs[:4]
    out_refs = refs[4:]
    rows = theirs_ref.shape[0]
    mine = mine_ref[start : start + rows]
    theirs = theirs_ref[...]
    for out_ref, block in zip(out_refs, column_blocks(steps)):
        columns = pl.ds(pl.multiple_of(block * 512, 512), 512)
        total = jnp.dot(mine, own_ref[:, columns], preferred_element_type=jnp.float32)
        total += jnp.dot(theirs, got_ref[:, columns], preferred_element_type=jnp.float32)
        out_ref[...] = total.astype(jnp.bfloat16)


def project(steps, start, mine, theirs, own, got):
    count = len(steps)
    out = jax.ShapeDtypeStruct(theirs.shape, jnp.bfloat16)
    return call(
        functools.partial(project_kernel, steps, start), count, [out] * count, mine, theirs, own, got
    )


def finish_kernel(*refs):
    inputs, (out_ref, total_ref, sems) = refs[:-3], refs[-3:]
    near = lax.axis_index("tp") // 4
    count = len(PARTS)
    copies = []
    start = 0
    for part, rows in enumerate(PARTS):
        swapped = inputs[count + part * 3 + 2]
        there = pl.multiple_of((1 - near) * sum(PARTS) + start, CHUNK)
        copies.append(
            pltpu.make_async_copy(swapped, out_ref.at[pl.ds(there, rows)], sems.at[part, 0])
        )
        copies[-1].start()
        start += rows
    start = 0
    for part, rows in enumerate(PARTS):
        own, (right, left) = inputs[part], inputs[count + part * 3 : count + part * 3 + 2]
        total = own[...].astype(jnp.float32) + right[...].astype(jnp.float32)
        mine = total_ref.at[start : start + rows]
        mine[...] = (total + left[...].astype(jnp.float32)).astype(jnp.bfloat16)
        here = pl.multiple_of(near * sum(PARTS) + start, CHUNK)
        copies.append(
            pltpu.make_async_copy(mine, out_ref.at[pl.ds(here, rows)], sems.at[part, 1])
        )
        copies[-1].start()
        start += rows
    for copy in copies:
        copy.wait()


def plus(*arrays):
    total = arrays[0].astype(jnp.float32)
    for array in arrays[1:]:
        total = total + array.astype(jnp.float32)
    return total.astype(jnp.bfloat16)


def layer(query, keys, values, residues, rates, w_out):
    length, width = keys.shape
    shape = jax.ShapeDtypeStruct

    modes = jnp.concatenate([rates.T, residues.T])
    shared, common = cut_slabs(w_out)
    shared = move(shared, either_side)
    common = move(common, either_side)
    fetched = [
        shared,
        move(shared[: SHARED // 2], along("y", 4, 1)),
        move(shared[SHARED // 2 :], along("y", 4, -1)),
        common,
    ]

    small = shape((STATE, width), jnp.float32)
    states, last, spread, leaving, taps, product = call(
        state_kernel,
        3,
        (
            shape((length // CHUNK * STATE, width), jnp.float32),
            small,
            small,
            shape((CHUNK, width), jnp.bfloat16),
            shape((width // SHARE * CHUNK, CHUNK), jnp.bfloat16),
            shape(keys.shape, jnp.bfloat16),
        ),
        modes, keys, values,
    )
    near = []
    for k in range(1, 4):
        pairs = [(c, c ^ k) for c in range(16)]
        near.append(lax.ppermute(last, "ctx", pairs))
    total, before, spread = call(join_kernel, 1, (small, small, small), spread, last, *near)
    above = [
        lax.ppermute(total, "ctx", [(c, c + 4 * k) for c in range(16 - 4 * k)])
        for k in range(1, 4)
    ]
    tall = shape((length // 2, width), jnp.bfloat16)
    turned = pltpu.VMEM((width // LANES, LANES, length // 2), jnp.bfloat16)
    local = call(near_kernel, 3, tall, taps, product, scratch=[turned])
    above, local = lax.optimization_barrier((above, local))
    others = call(
        send_kernel, 2, [shape((rows, width), jnp.bfloat16) for rows in PARTS],
        spread, leaving, query, local, states, before, *above,
    )
    theirs = [move(other, along("near", 2, 1)) for other in others]
    mine = call(
        keep_kernel, 4, tall,
        spread, leaving, query, taps, product, states, before, *above,
        scratch=[turned, pltpu.VMEM((length // 2, width), jnp.bfloat16)],
    )
    common, others = lax.optimization_barrier((common, others))
    fetched[3] = common
    swapped = [move(piece, along("core", 2, 1)) for piece in fetched]
    pieces = fetched + swapped
    got = gather(pieces)

    finals, rest = [], []
    for part in range(len(PARTS)):
        start = sum(PARTS[:part])
        if part:
            theirs[part], free = lax.optimization_barrier((theirs[part], free))
        args = (start, mine, theirs[part], w_out, got)
        far = ((2, True), (2, False))
        near_free = ((1, False), (-1, True))
        rest_steps = ((1, True), (-1, False), (0, True), (0, False))
        first = far if part else far + near_free
        last_ones = near_free + rest_steps if part else rest_steps
        blocks = project(first, *args)
        blocks += project(last_ones, *args)
        far_p, far_o, right_o, left_p, right_p, left_o, own_p, own_o = blocks
        finals.append(own_o)
        free = right_o
        far_p = move(far_p, along("z", 4, 1))
        far_o = move(far_o, along("z", 4, -1))
        right_o = move(right_o, along("z", 4, 1))
        left_p = move(left_p, along("z", 4, -1))
        right_p = move(plus(right_p, far_p), along("z", 4, 1))
        left_o = move(plus(left_o, far_o), along("z", 4, -1))
        swapped = move(plus(own_p, right_p, left_p), along("near", 2, 1))
        rest += [right_o, left_o, swapped]
    return pl.pallas_call(
        finish_kernel,
        out_shape=shape((length, 512), jnp.bfloat16),
        in_specs=[vmem()] * (len(finals) + len(rest)),
        out_specs=anywhere(),
        scratch_shapes=[
            pltpu.VMEM((sum(PARTS), 512), jnp.bfloat16),
            pltpu.SemaphoreType.DMA((len(PARTS), 2)),
        ],
        cost_estimate=cost(1),
        compiler_params=pltpu.CompilerParams(vmem_limit_bytes=LIMIT),
    )(*finals, *rest)


def solution(mesh):
    in_specs = (P("ctx", "tp"), P("ctx", "tp"), P("ctx", "tp"), P(), P(), P("tp", None))
    return jax.shard_map(
        layer, mesh=mesh, in_specs=in_specs, out_specs=P("ctx", "tp"), check_vma=False
    )
```
